32 devices in a mesh: ctx: 16 (over z, x, core), tp: 2 (over y).
Axes of the slice: x: 2, y: 2, z: 4, core: 2. Of those that a mesh axis runs over, the one named last changes fastest.
Arguments:
- token_ids: int32 [8192], P('ctx'), may hold values from 0 to 511
- embed_table: bfloat16 [512, 8192], P(None, 'tp'), may hold values from -81 to 81
- projected_table: bfloat16 [512, 3, 8192], P(None, None, 'tp'), may hold values from -10.5 to 10.5
- feat_one: float32 [3, 3, 8192], P(None, None, 'tp'), may hold values from -3 to 3
- inner_taps: float32 [7, 8192], P(None, 'tp'), may hold values from -2 to 2
- feat_two: float32 [3, 3, 8192], P(None, None, 'tp'), may hold values from -3 to 3
- decay: float32 [8192, 16], P('tp'), may hold values from 3.540039e-05 to 0.03448276
- residue: float32 [8192, 16], P('tp'), may hold values from -0.26261287 to 0.26261287
Outputs:
- stream_out: bfloat16 [8192, 8192], P('ctx', 'tp')
The draws below stay inside these ranges and needn't reach their ends.
All inputs are finite; a program needn't handle non-finite values.
Results may differ from the reference program's by a relative error of at most 0.0048.
Values may be sent and summed in bfloat16 or wider, within the bound.
A program may use at most 320 MiB of HBM per device.

```python
import math
import jax
import jax.numpy as jnp
import numpy as np
from jax import lax

D = 8192
VOCAB = 512
FEAT_TAPS = 3
SHORT_TAPS = 7
MODES = 16
TOKENS = 8192


def draw_embed_table(key, part):
    subkeys = jax.random.split(jax.random.fold_in(key, 11), 3)
    column = jnp.arange(D, dtype=jnp.int32).astype(jnp.float32)
    rising = 4.0 ** (column / D - 0.5)
    row_scale = jnp.exp(jax.random.uniform(subkeys[1], (VOCAB, 1), jnp.float32) * math.log(10.0))
    col_scale = jnp.exp(jax.random.uniform(subkeys[2], (1, D), jnp.float32) * math.log(10.0))
    entries = jnp.clip(jax.random.normal(subkeys[0], (VOCAB, D), jnp.float32), -4.0, 4.0)
    return (entries * row_scale * col_scale * rising[None, :] / 10.0).astype(jnp.bfloat16)


def draw_projected_table(key, part):
    subkeys = jax.random.split(jax.random.fold_in(key, 23), 3)
    row_scale = jnp.exp(jax.random.uniform(subkeys[1], (VOCAB, 1, 1), jnp.float32, math.log(0.6), math.log(1.6)))
    col_scale = jnp.exp(jax.random.uniform(subkeys[2], (1, 3, D), jnp.float32, math.log(0.6), math.log(1.6)))
    entries = jnp.clip(jax.random.normal(subkeys[0], (VOCAB, 3, D), jnp.float32), -4.0, 4.0)
    return (entries * row_scale * col_scale).astype(jnp.bfloat16)


def mode_draw(key):
    subkeys = jax.random.split(jax.random.fold_in(key, 37), 4)
    slow_share = 0.5
    chooser = jax.random.uniform(subkeys[0], (D, 1), jnp.float32)
    slow_rates = jnp.exp(jax.random.uniform(subkeys[1], (D, MODES), jnp.float32, math.log(0.3 / TOKENS), math.log(2.0 / TOKENS)))
    fast_rates = jnp.exp(jax.random.uniform(subkeys[2], (D, MODES), jnp.float32, math.log(1.0 / 50.0), math.log(1.0 / 30.0)))
    decays = jnp.where(chooser < slow_share, slow_rates, fast_rates)
    weights = jnp.clip(jax.random.normal(subkeys[3], (D, MODES), jnp.float32), -4.0, 4.0) * jnp.sqrt(2.0 * decays / MODES)
    return (decays, weights)


def draw_decay(key, part):
    return mode_draw(key)[0]


def draw_residue(key, part):
    return mode_draw(key)[1]


def set_ends(values, own_key, low, largest):
    longest = values.shape.index(max(values.shape))
    spots = []
    for shift in (0, 1):
        where = [jax.random.randint(jax.random.fold_in(own_key, axis), (), 0, length) for axis, length in enumerate(values.shape)]
        where[longest] = (where[longest] + shift) % values.shape[longest]
        spots.append(tuple(where))
    return values.at[spots[0]].set(low).at[spots[1]].set(largest)


def steps_of(key, extent, cuts, smallest, largest):
    def one(axis_at, parts):
        draws = jax.random.uniform(jax.random.fold_in(jax.random.fold_in(key, 6), axis_at), (parts,), jnp.float32, smallest / len(cuts), largest / len(cuts))
        return jnp.repeat(jnp.exp(draws), extent[axis_at] // parts).reshape((-1,) + (1,) * (len(extent) - axis_at - 1))

    loudness = one(*cuts[0])
    for cut in cuts[1:]:
        loudness = loudness * one(*cut)
    return loudness


def cumulative_ranks(amount, slope):
    portions = [(1 << 20) // math.isqrt(grade ** slope) + 1 for grade in range(1, amount + 1)]
    width = 1 + sum(portions) // (1 << 30)
    return np.cumsum(np.array([max(1, weight // width) for weight in portions]))


def skewed_ids(stream_key, extent, number_of, skew):
    listing = cumulative_ranks(number_of, skew)
    ticket = jax.random.randint(jax.random.fold_in(stream_key, 1), extent, 0, int(listing[number_of - 1]))
    rank = jnp.searchsorted(jnp.asarray(listing, jnp.int32), ticket, side="right")
    return jax.random.permutation(jax.random.fold_in(stream_key, 2), number_of)[rank].astype(jnp.int32)


def centred(own_key, dims, deviation, limit, cuts=(), kind=jnp.bfloat16):
    values = jax.random.normal(own_key, dims, jnp.float32) * deviation
    if len(cuts) > 0:
        values = steps_of(own_key, dims, cuts, -0.22, 0.18) * values
    return jnp.clip(values, min=-limit, max=limit).astype(kind)


def setup_inputs(seed: int = 0) -> dict:
    arg_keys = jax.random.split(jax.random.key(seed), 9)
    return {
        "token_ids": set_ends(skewed_ids(arg_keys[0], (TOKENS,), VOCAB, 2), jax.random.fold_in(arg_keys[0], 3), 0, VOCAB - 1).astype(jnp.int32),
        "embed_table": draw_embed_table(jax.random.fold_in(arg_keys[8], 71), 0),
        "projected_table": draw_projected_table(jax.random.fold_in(arg_keys[8], 71), 0),
        "feat_one": centred(arg_keys[3], (FEAT_TAPS, 3, D), 0.6, 3.0, ((2, 2),), jnp.float32),
        "inner_taps": centred(arg_keys[4], (SHORT_TAPS, D), 0.4, 2.0, ((1, 2),), jnp.float32),
        "feat_two": centred(arg_keys[5], (FEAT_TAPS, 3, D), 0.6, 3.0, ((2, 2),), jnp.float32),
        "decay": draw_decay(jax.random.fold_in(arg_keys[8], 71), 0),
        "residue": draw_residue(jax.random.fold_in(arg_keys[8], 71), 0),
    }


epsilon = 1e-06

def causal_taps(series, weights):
    tap_count = weights.shape[0]
    length = series.shape[0]
    padded = jnp.concatenate([jnp.zeros((tap_count - 1,) + series.shape[1:], series.dtype), series], axis=0)
    summed = jnp.zeros_like(series)
    for offset in range(tap_count):
        summed = summed + weights[offset] * padded[tap_count - 1 - offset:tap_count - 1 - offset + length]
    return summed

def by_blocks(array, axis, blocks):
    reordered = jnp.moveaxis(array, axis, -1)
    reordered = reordered.reshape(reordered.shape[:-1] + (blocks, reordered.shape[-1] // blocks))
    return jnp.moveaxis(reordered, -2, 0)

def reference(token_ids, embed_table, projected_table, feat_one, inner_taps, feat_two, decay, residue):
    blocks = 16
    length = token_ids.shape[0]
    positions = jnp.arange(length).astype(jnp.float32)

    def first_block(pieces):
        emb_piece, proj_piece, feat_piece, inner_piece = pieces
        embedded = jnp.take(emb_piece, token_ids, axis=0).astype(jnp.float32)
        raw_rows = jnp.take(proj_piece, token_ids, axis=0).astype(jnp.float32)
        queries = causal_taps(raw_rows[:, 0], feat_piece[:, 0])
        key_rows = causal_taps(raw_rows[:, 1], feat_piece[:, 1])
        valued = causal_taps(raw_rows[:, 2], feat_piece[:, 2])
        return (embedded + queries * causal_taps(key_rows * valued, inner_piece)).astype(jnp.bfloat16)
    stream = lax.map(first_block, (by_blocks(embed_table, 1, blocks), by_blocks(projected_table, 2, blocks), by_blocks(feat_one, 2, blocks), by_blocks(inner_taps, 1, blocks)))
    stream = jnp.moveaxis(stream, 0, 1).reshape(length, D)
    widened = stream.astype(jnp.float32)
    inverse_rms = lax.rsqrt(lax.optimization_barrier(jnp.sum(widened * widened, axis=1)) / D + epsilon)

    def second_block(pieces):
        stream_piece, feat_piece, decay_piece, residue_piece = pieces
        normed = stream_piece.astype(jnp.float32) * inverse_rms[:, None]
        queries = causal_taps(normed, feat_piece[:, 0])
        key_rows = causal_taps(normed, feat_piece[:, 1])
        valued = causal_taps(normed, feat_piece[:, 2])
        product = lax.optimization_barrier((key_rows * valued).astype(jnp.bfloat16)).astype(jnp.float32)
        response = jnp.zeros_like(normed)
        for mode_number in range(decay_piece.shape[0]):
            response = response + residue_piece[mode_number] * jnp.exp(-decay_piece[mode_number] * positions[:, None])
        padded_len = 2 * length
        spectrum = jnp.fft.rfft(product, n=padded_len, axis=0) * jnp.fft.rfft(response, n=padded_len, axis=0)
        convolved = jnp.fft.irfft(spectrum, n=padded_len, axis=0)[:length]
        return (stream_piece.astype(jnp.float32) + queries * convolved).astype(jnp.bfloat16)
    result = lax.map(second_block, (by_blocks(stream, 1, blocks), by_blocks(feat_two, 2, blocks), by_blocks(decay, 0, blocks), by_blocks(residue, 0, blocks)))
    return jnp.moveaxis(result, 0, 1).reshape(length, D)
```

```python
import functools

import jax
import jax.numpy as jnp
from jax import lax
from jax.experimental import pallas as pl
from jax.experimental.pallas import tpu as pltpu
from jax.sharding import PartitionSpec as P

epsilon = 1e-06
HALO = 16
SEGMENTS = 8
LANES = 128
VMEM_LIMIT = 60 * 1024 * 1024


def shifted(value, axis, steps):
    count = lax.axis_size(axis)
    return lax.ppermute(value, axis, [(source, source + steps) for source in range(count - steps)])


def rolled_taps(series, taps):
    summed = taps[0] * series
    for offset in range(1, len(taps)):
        summed = summed + taps[offset] * pltpu.roll(series, offset, 0)
    return summed


def block_rows(rows):
    chunk = 128 if (rows - HALO) % 128 == 0 else rows - HALO
    spans = [(0, 0, HALO)]
    spans += [(start - HALO, start, chunk) for start in range(HALO, rows, chunk)]
    return spans


def first_kernel(one_hot, embed, proj, feat, inner, stream, squares, raw):
    rows = one_hot.shape[0]
    width = embed.shape[1]
    ids = one_hot[...]
    raw[0] = jnp.dot(ids, embed[...], preferred_element_type=jnp.float32)
    for s in range(3):
        raw[1 + s] = jnp.dot(ids, proj[s], preferred_element_type=jnp.float32)

    @pl.when(pl.program_id(0) == 0)
    def _():
        squares[...] = jnp.zeros_like(squares)

    @pl.loop(0, width // LANES)
    def _(block):
        lanes = pl.ds(pl.multiple_of(block * LANES, LANES), LANES)
        feat_taps = [[feat[j, s : s + 1, lanes] for j in range(feat.shape[0])] for s in range(3)]
        inner_taps = [inner[j : j + 1, lanes] for j in range(inner.shape[0])]
        for base, start, count in block_rows(rows):
            slab = pl.ds(base, start - base + count)
            queries = rolled_taps(raw[1, slab, lanes], feat_taps[0])
            keyed = rolled_taps(raw[2, slab, lanes], feat_taps[1])
            valued = rolled_taps(raw[3, slab, lanes], feat_taps[2])
            mixture = rolled_taps(keyed * valued, inner_taps)
            total = (raw[0, slab, lanes] + queries * mixture)[start - base :].astype(jnp.bfloat16)
            stream[pl.ds(start, count), lanes] = total
            wide = total.astype(jnp.float32)
            squares[pl.ds(start, count), :] += wide * wide


def second_kernel(stream, inverse, feat, rate, product, states, series):
    rows = stream.shape[0]
    width = stream.shape[1]
    steps = (rows - HALO) // SEGMENTS
    modes = rate.shape[0]
    for block in range(width // LANES):
        lanes = slice(block * LANES, (block + 1) * LANES)
        taps = [[feat[j, s : s + 1, lanes] for j in range(feat.shape[0])] for s in (1, 2)]
        for base, start, count in block_rows(rows)[1:]:
            slab = pl.ds(base, start - base + count)
            normed = stream[slab, lanes].astype(jnp.float32) * inverse[slab, :]
            both = rolled_taps(normed, taps[0]) * rolled_taps(normed, taps[1])
            rounded = both[start - base :].astype(jnp.bfloat16)
            product[pl.ds(start - HALO, count), lanes] = rounded
            series[block, pl.ds(start - HALO, count), :] = rounded.astype(jnp.float32)
        rates = [jnp.broadcast_to(rate[m : m + 1, lanes], (SEGMENTS, LANES)) for m in range(modes)]

        def step(at, held):
            value = series[block, pl.ds(at, SEGMENTS, stride=steps), :]
            return tuple(rates[m] * held[m] + value for m in range(modes))

        zero = jnp.zeros((SEGMENTS, LANES), jnp.float32)
        held = lax.fori_loop(0, steps, step, (zero,) * modes, unroll=4)
        for m in range(modes):
            states[m, :, lanes] = held[m]


def third_kernel(stream, inverse, feat, rate, weight, product, states, out, series, result):
    rows = stream.shape[0]
    width = stream.shape[1]
    steps = (rows - HALO) // SEGMENTS
    modes = rate.shape[0]
    for block in range(width // LANES):
        lanes = slice(block * LANES, (block + 1) * LANES)
        series[block] = product[:, lanes].astype(jnp.float32)
        rates = [jnp.broadcast_to(rate[m : m + 1, lanes], (SEGMENTS, LANES)) for m in range(modes)]
        weights = [
            jnp.broadcast_to(weight[m : m + 1, lanes], (SEGMENTS, LANES)) for m in range(modes)
        ]

        def step(at, held):
            where = pl.ds(at, SEGMENTS, stride=steps)
            value = series[block, where, :]
            held = tuple(rates[m] * held[m] + value for m in range(modes))
            terms = [weights[m] * held[m] for m in range(modes)]
            while len(terms) > 1:
                pairs = [a + b for a, b in zip(terms[::2], terms[1::2])]
                terms = pairs + terms[2 * len(pairs) :]
            result[block, where, :] = terms[0]
            return held

        first = tuple(states[m, :, lanes] for m in range(modes))
        lax.fori_loop(0, steps, step, first, unroll=4)
        taps = [feat[j, 0:1, lanes] for j in range(feat.shape[0])]
        for base, start, count in block_rows(rows)[1:]:
            slab = pl.ds(base, start - base + count)
            wide = stream[slab, lanes].astype(jnp.float32)
            queries = rolled_taps(wide * inverse[slab, :], taps)[start - base :]
            convolved = result[block, pl.ds(start - HALO, count), :]
            total = wide[start - base :] + queries * convolved
            out[pl.ds(start - HALO, count), lanes] = total.astype(jnp.bfloat16)


def on_device(
    token_ids, embed_table, projected_table, feat_one, inner_taps, feat_two, decay, residue
):
    tokens = token_ids.shape[0]
    vocab, channels = embed_table.shape
    modes = decay.shape[1]
    rows = tokens + HALO
    count = lax.axis_size("ctx")
    all_channels = channels * lax.axis_size("tp")
    params = pltpu.CompilerParams(
        dimension_semantics=("arbitrary",), vmem_limit_bytes=VMEM_LIMIT
    )

    earlier = shifted(token_ids[tokens - HALO :] + 1, "ctx", 1) - 1
    ids = jnp.concatenate([earlier, token_ids])
    one_hot = (ids[:, None] == jnp.arange(vocab, dtype=jnp.int32)[None, :]).astype(jnp.bfloat16)
    proj = jnp.transpose(projected_table, (1, 0, 2))

    wide = min(512, channels)
    feat_spec = lambda size: pl.BlockSpec((feat_one.shape[0], 3, size), lambda c: (0, 0, c))
    stream, squares = pl.pallas_call(
        first_kernel,
        grid=(channels // wide,),
        in_specs=[
            pl.BlockSpec((rows, vocab), lambda c: (0, 0)),
            pl.BlockSpec((vocab, wide), lambda c: (0, c)),
            pl.BlockSpec((3, vocab, wide), lambda c: (0, 0, c)),
            feat_spec(wide),
            pl.BlockSpec((inner_taps.shape[0], wide), lambda c: (0, c)),
        ],
        out_specs=[
            pl.BlockSpec((rows, wide), lambda c: (0, c)),
            pl.BlockSpec((rows, LANES), lambda c: (0, 0)),
        ],
        out_shape=[
            jax.ShapeDtypeStruct((rows, channels), jnp.bfloat16),
            jax.ShapeDtypeStruct((rows, LANES), jnp.float32),
        ],
        scratch_shapes=[pltpu.VMEM((4, rows, wide), jnp.float32)],
        compiler_params=params,
        name="first_block",
    )(one_hot, embed_table, proj, feat_one, inner_taps)

    summed = lax.psum(jnp.sum(squares, axis=1), "tp")
    inverse = lax.rsqrt(summed / all_channels + epsilon)
    inverse = jnp.broadcast_to(inverse[:, None], (rows, LANES))

    slope = jnp.transpose(decay)
    weight = jnp.transpose(residue)
    rate = jnp.exp(-slope)
    size = min(256, channels)
    blocks = size // LANES
    stream_spec = pl.BlockSpec((rows, size), lambda c: (0, c))
    inverse_spec = pl.BlockSpec((rows, LANES), lambda c: (0, 0))
    mode_spec = pl.BlockSpec((modes, size), lambda c: (0, c))
    token_spec = pl.BlockSpec((tokens, size), lambda c: (0, c))
    state_spec = pl.BlockSpec((modes, SEGMENTS, size), lambda c: (0, 0, c))
    product, states = pl.pallas_call(
        second_kernel,
        grid=(channels // size,),
        in_specs=[stream_spec, inverse_spec, feat_spec(size), mode_spec],
        out_specs=[token_spec, state_spec],
        out_shape=[
            jax.ShapeDtypeStruct((tokens, channels), jnp.bfloat16),
            jax.ShapeDtypeStruct((modes, SEGMENTS, channels), jnp.float32),
        ],
        scratch_shapes=[pltpu.VMEM((blocks, tokens, LANES), jnp.float32)],
        compiler_params=params,
        name="local_states",
    )(stream, inverse, feat_two, rate)

    per_segment = jnp.exp(-slope * float(tokens // SEGMENTS))
    whole = states[:, 0]
    for s in range(1, SEGMENTS):
        whole = per_segment * whole + states[:, s]
    spread = lax.all_to_all(whole, "ctx", split_axis=1, concat_axis=0, tiled=True)
    spread = spread.reshape(count, modes, channels // count)
    share = channels // count
    mine = lax.dynamic_slice_in_dim(slope, lax.axis_index("ctx") * share, share, 1)
    per_shard = jnp.exp(-mine * float(tokens))
    carry = jnp.zeros((modes, share), jnp.float32)
    carries = []
    for s in range(count):
        carries.append(carry)
        carry = per_shard * carry + spread[s]
    carried = jnp.concatenate(carries, axis=0)
    start = lax.all_to_all(carried, "ctx", split_axis=0, concat_axis=1, tiled=True)
    starts = [start]
    for s in range(SEGMENTS - 1):
        starts.append(per_segment * starts[-1] + states[:, s])
    entering = jnp.stack(starts, axis=1)

    return pl.pallas_call(
        third_kernel,
        grid=(channels // size,),
        in_specs=[
            stream_spec,
            inverse_spec,
            feat_spec(size),
            mode_spec,
            mode_spec,
            token_spec,
            state_spec,
        ],
        out_specs=token_spec,
        out_shape=jax.ShapeDtypeStruct((tokens, channels), jnp.bfloat16),
        scratch_shapes=[
            pltpu.VMEM((blocks, tokens, LANES), jnp.float32),
            pltpu.VMEM((blocks, tokens, LANES), jnp.float32),
        ],
        compiler_params=params,
        name="long_convolution",
    )(stream, inverse, feat_two, rate, weight, product, entering)


def solution(mesh):
    placed = (
        P("ctx"),
        P(None, "tp"),
        P(None, None, "tp"),
        P(None, None, "tp"),
        P(None, "tp"),
        P(None, None, "tp"),
        P("tp", None),
        P("tp", None),
    )
    return jax.shard_map(
        on_device, mesh=mesh, in_specs=placed, out_specs=P("ctx", "tp"), check_vma=False
    )
```

```python
import functools

import jax
import jax.numpy as jnp
from jax import lax
from jax.experimental import pallas as pl
from jax.experimental.pallas import tpu as pltpu
from jax.sharding import PartitionSpec as P

epsilon = 1e-06
HALO = 16
SEGMENTS = 8
LANES = 128
VMEM_LIMIT = 60 * 1024 * 1024


def shifted(value, axis, steps):
    count = lax.axis_size(axis)
    return lax.ppermute(value, axis, [(source, source + steps) for source in range(count - steps)])


def rolled_taps(series, taps):
    summed = taps[0] * series
    for offset in range(1, len(taps)):
        summed = summed + taps[offset] * pltpu.roll(series, offset, 0)
    return summed


def block_rows(rows):
    chunk = 128 if (rows - HALO) % 128 == 0 else rows - HALO
    spans = [(0, 0, HALO)]
    spans += [(start - HALO, start, chunk) for start in range(HALO, rows, chunk)]
    return spans


def first_kernel(one_hot, embed, proj, feat, inner, stream, squares, raw):
    rows = one_hot.shape[0]
    width = embed.shape[1]
    ids = one_hot[...]
    raw[0] = jnp.dot(ids, embed[...], preferred_element_type=jnp.float32)
    for s in range(3):
        raw[1 + s] = jnp.dot(ids, proj[s], preferred_element_type=jnp.float32)

    @pl.when(pl.program_id(0) == 0)
    def _():
        squares[...] = jnp.zeros_like(squares)

    @pl.loop(0, width // LANES)
    def _(block):
        lanes = pl.ds(pl.multiple_of(block * LANES, LANES), LANES)
        feat_taps = [[feat[j, s : s + 1, lanes] for j in range(feat.shape[0])] for s in range(3)]
        inner_taps = [inner[j : j + 1, lanes] for j in range(inner.shape[0])]
        for base, start, count in block_rows(rows):
            slab = pl.ds(base, start - base + count)
            queries = rolled_taps(raw[1, slab, lanes], feat_taps[0])
            keyed = rolled_taps(raw[2, slab, lanes], feat_taps[1])
            valued = rolled_taps(raw[3, slab, lanes], feat_taps[2])
            mixture = rolled_taps(keyed * valued, inner_taps)
            total = (raw[0, slab, lanes] + queries * mixture)[start - base :].astype(jnp.bfloat16)
            stream[pl.ds(start, count), lanes] = total
            wide = total.astype(jnp.float32)
            squares[pl.ds(start, count), :] += wide * wide


def segment_scan(first, local, slope, steps):
    place = lax.broadcasted_iota(jnp.int32, (SEGMENTS, LANES), 0)
    total = jnp.where(place == 0, first, pltpu.roll(local, 1, 0))
    reach = 1
    while reach < SEGMENTS:
        factor = jnp.exp(slope * float(-steps * reach))
        total = total + jnp.where(place >= reach, factor * pltpu.roll(total, reach, 0), 0.0)
        reach *= 2
    return total


def second_kernel(stream, inverse, feat, slope, product, states, whole, series, ends):
    rows = stream.shape[0]
    width = stream.shape[1]
    steps = (rows - HALO) // SEGMENTS
    modes = slope.shape[0]
    place = lax.broadcasted_iota(jnp.int32, (SEGMENTS, LANES), 0)
    ahead = ((place - (SEGMENTS - 1)) * steps).astype(jnp.float32)
    for block in range(width // LANES):
        lanes = slice(block * LANES, (block + 1) * LANES)
        taps = [[feat[j, s : s + 1, lanes] for j in range(feat.shape[0])] for s in (1, 2)]
        for base, start, count in block_rows(rows)[1:]:
            slab = pl.ds(base, start - base + count)
            normed = stream[slab, lanes].astype(jnp.float32) * inverse[slab, :]
            both = rolled_taps(normed, taps[0]) * rolled_taps(normed, taps[1])
            rounded = both[start - base :].astype(jnp.bfloat16)
            product[pl.ds(start - HALO, count), lanes] = rounded
            series[block, pl.ds(start - HALO, count), :] = rounded.astype(jnp.float32)
        rate = jnp.exp(-slope[:, lanes])
        rates = [jnp.broadcast_to(rate[m : m + 1], (SEGMENTS, LANES)) for m in range(modes)]

        def step(at, held):
            value = series[block, pl.ds(at, SEGMENTS, stride=steps), :]
            return tuple(rates[m] * held[m] + value for m in range(modes))

        zero = jnp.zeros((SEGMENTS, LANES), jnp.float32)
        held = lax.fori_loop(0, steps, step, (zero,) * modes, unroll=4)
        for m in range(modes):
            states[m, :, lanes] = held[m]
            scaled = held[m] * jnp.exp(slope[m : m + 1, lanes] * ahead)
            ends[m : m + 1, :] = jnp.sum(scaled, axis=0, keepdims=True)
        whole[0, :, lanes] = ends[...].astype(whole.dtype)


def third_kernel(
    stream, inverse, feat, slope, weight, product, states, entering, out, series, result
):
    rows = stream.shape[0]
    width = stream.shape[1]
    steps = (rows - HALO) // SEGMENTS
    modes = slope.shape[0]
    for block in range(width // LANES):
        lanes = slice(block * LANES, (block + 1) * LANES)
        series[block] = product[:, lanes].astype(jnp.float32)
        rate = jnp.exp(-slope[:, lanes])
        rates = [jnp.broadcast_to(rate[m : m + 1], (SEGMENTS, LANES)) for m in range(modes)]
        weights = [
            jnp.broadcast_to(weight[m : m + 1, lanes], (SEGMENTS, LANES)) for m in range(modes)
        ]

        def step(at, held):
            where = pl.ds(at, SEGMENTS, stride=steps)
            value = series[block, where, :]
            held = tuple(rates[m] * held[m] + value for m in range(modes))
            terms = [weights[m] * held[m] for m in range(modes)]
            while len(terms) > 1:
                pairs = [a + b for a, b in zip(terms[::2], terms[1::2])]
                terms = pairs + terms[2 * len(pairs) :]
            result[block, where, :] = terms[0]
            return held

        arriving = entering[0, :, lanes].astype(jnp.float32)
        first = tuple(
            segment_scan(arriving[m : m + 1], states[m, :, lanes], slope[m : m + 1, lanes], steps)
            for m in range(modes)
        )
        lax.fori_loop(0, steps, step, first, unroll=4)
        taps = [feat[j, 0:1, lanes] for j in range(feat.shape[0])]
        for base, start, count in block_rows(rows)[1:]:
            slab = pl.ds(base, start - base + count)
            wide = stream[slab, lanes].astype(jnp.float32)
            queries = rolled_taps(wide * inverse[slab, :], taps)[start - base :]
            convolved = result[block, pl.ds(start - HALO, count), :]
            total = wide[start - base :] + queries * convolved
            out[pl.ds(start - HALO, count), lanes] = total.astype(jnp.bfloat16)


def regrouped(value, groups):
    if value.shape[0] == groups:
        return value
    modes = value.shape[1]
    flat = jnp.transpose(value, (1, 0, 2)).reshape(modes, groups, -1)
    return jnp.transpose(flat, (1, 0, 2))


def on_device(
    token_ids, embed_table, projected_table, feat_one, inner_taps, feat_two, decay, residue
):
    tokens = token_ids.shape[0]
    vocab, channels = embed_table.shape
    modes = decay.shape[1]
    rows = tokens + HALO
    count = lax.axis_size("ctx")
    all_channels = channels * lax.axis_size("tp")
    params = pltpu.CompilerParams(
        dimension_semantics=("arbitrary",), vmem_limit_bytes=VMEM_LIMIT
    )

    earlier = shifted(token_ids[tokens - HALO :] + 1, "ctx", 1) - 1
    ids = jnp.concatenate([earlier, token_ids])
    one_hot = (ids[:, None] == jnp.arange(vocab, dtype=jnp.int32)[None, :]).astype(jnp.bfloat16)
    proj = jnp.transpose(projected_table, (1, 0, 2))

    wide = min(512, channels)
    feat_spec = lambda size: pl.BlockSpec((feat_one.shape[0], 3, size), lambda c: (0, 0, c))
    stream, squares = pl.pallas_call(
        first_kernel,
        grid=(channels // wide,),
        in_specs=[
            pl.BlockSpec((rows, vocab), lambda c: (0, 0)),
            pl.BlockSpec((vocab, wide), lambda c: (0, c)),
            pl.BlockSpec((3, vocab, wide), lambda c: (0, 0, c)),
            feat_spec(wide),
            pl.BlockSpec((inner_taps.shape[0], wide), lambda c: (0, c)),
        ],
        out_specs=[
            pl.BlockSpec((rows, wide), lambda c: (0, c)),
            pl.BlockSpec((rows, LANES), lambda c: (0, 0)),
        ],
        out_shape=[
            jax.ShapeDtypeStruct((rows, channels), jnp.bfloat16),
            jax.ShapeDtypeStruct((rows, LANES), jnp.float32),
        ],
        scratch_shapes=[pltpu.VMEM((4, rows, wide), jnp.float32)],
        compiler_params=params,
        name="first_block",
    )(one_hot, embed_table, proj, feat_one, inner_taps)

    summed = lax.psum(jnp.sum(squares, axis=1), "tp")
    inverse = lax.rsqrt(summed / all_channels + epsilon)
    inverse = jnp.broadcast_to(inverse[:, None], (rows, LANES))

    slope = jnp.transpose(decay)
    weight = jnp.transpose(residue)
    share = channels // count
    size = share if share % LANES == 0 and share <= 512 else min(256, channels)
    groups = channels // size
    blocks = size // LANES
    stream_spec = pl.BlockSpec((rows, size), lambda c: (0, c))
    inverse_spec = pl.BlockSpec((rows, LANES), lambda c: (0, 0))
    mode_spec = pl.BlockSpec((modes, size), lambda c: (0, c))
    token_spec = pl.BlockSpec((tokens, size), lambda c: (0, c))
    state_spec = pl.BlockSpec((modes, SEGMENTS, size), lambda c: (0, 0, c))
    whole_spec = pl.BlockSpec((1, modes, size), lambda c: (c, 0, 0))
    product, states, whole = pl.pallas_call(
        second_kernel,
        grid=(channels // size,),
        in_specs=[stream_spec, inverse_spec, feat_spec(size), mode_spec],
        out_specs=[token_spec, state_spec, whole_spec],
        out_shape=[
            jax.ShapeDtypeStruct((tokens, channels), jnp.bfloat16),
            jax.ShapeDtypeStruct((modes, SEGMENTS, channels), jnp.float32),
            jax.ShapeDtypeStruct((groups, modes, size), jnp.float32),
        ],
        scratch_shapes=[
            pltpu.VMEM((blocks, tokens, LANES), jnp.float32),
            pltpu.VMEM((modes, LANES), jnp.float32),
        ],
        compiler_params=params,
        name="local_states",
    )(stream, inverse, feat_two, slope)

    spread = lax.all_to_all(
        regrouped(whole, count), "ctx", split_axis=0, concat_axis=0, tiled=True
    ).astype(jnp.float32)
    mine = lax.dynamic_slice_in_dim(slope, lax.axis_index("ctx") * share, share, 1)
    per_shard = jnp.exp(-mine * float(tokens))
    carry = jnp.zeros((modes, share), jnp.float32)
    carries = []
    for s in range(count):
        carries.append(carry)
        carry = per_shard * carry + spread[s]
    entering = lax.all_to_all(
        jnp.stack(carries), "ctx", split_axis=0, concat_axis=0, tiled=True
    )
    entering = regrouped(entering, groups)

    return pl.pallas_call(
        third_kernel,
        grid=(channels // size,),
        in_specs=[
            stream_spec,
            inverse_spec,
            feat_spec(size),
            mode_spec,
            mode_spec,
            token_spec,
            state_spec,
            whole_spec,
        ],
        out_specs=token_spec,
        out_shape=jax.ShapeDtypeStruct((tokens, channels), jnp.bfloat16),
        scratch_shapes=[
            pltpu.VMEM((blocks, tokens, LANES), jnp.float32),
            pltpu.VMEM((blocks, tokens, LANES), jnp.float32),
        ],
        compiler_params=params,
        name="long_convolution",
    )(stream, inverse, feat_two, slope, weight, product, states, entering)


def solution(mesh):
    placed = (
        P("ctx"),
        P(None, "tp"),
        P(None, None, "tp"),
        P(None, None, "tp"),
        P(None, "tp"),
        P(None, None, "tp"),
        P("tp", None),
        P("tp", None),
    )
    return jax.shard_map(
        on_device, mesh=mesh, in_specs=placed, out_specs=P("ctx", "tp"), check_vma=False
    )
```
